32 devices in a mesh: row: 8 (over z, core), col: 4 (over y, x).
Axes of the slice: x: 2, y: 2, z: 4, core: 2. Of those that a mesh axis runs over, the one named last changes fastest.
Arguments:
- view_left: bfloat16 [16384, 16384], P('row', 'col'), may hold values from -0.046875 to 0.046875
- view_right: bfloat16 [16384, 16384], P('row', 'col'), may hold values from -6 to 6
- view_product: bfloat16 [16384, 16384], P('row', 'col'), may hold values from -6 to 6
- delta_a_left: bfloat16 [16384, 512], P('row', 'col'), may hold values from -0.25 to 0.25
- delta_a_right: bfloat16 [16384, 512], P('row', 'col'), may hold values from -0.0625 to 0.0625
- delta_b_left: bfloat16 [16384, 512], P('col', 'row'), may hold values from -6 to 6
- delta_b_right: bfloat16 [16384, 512], P('col', 'row'), may hold values from -0.25 to 0.25
Outputs:
- updated_view: bfloat16 [16384, 16384], P('row', 'col')
The draws below stay inside these ranges and needn't reach their ends.
All inputs are finite; a program needn't handle non-finite values.
Results may differ from the reference program's by a relative error of at most 0.005.
Values may be sent and summed in bfloat16 or wider, within the bound.
No kernel may reach another device: no remote copies, remote signals or barrier semaphores. Data moves between devices by JAX's collectives and lax.ppermute only.
A program may use at most 192 MiB of HBM per device.

```python
import jax
import jax.numpy as jnp

N = 16384
R = 512


def spiked(array, stream_key, source, target, blocks, factor):
    def block_of(position):
        return (jnp.arange(array.shape[position]) // (array.shape[position] // blocks)).reshape((-1,) + (1,) * (array.ndim - 1 - position))

    near = jax.random.permutation(stream_key, blocks)[block_of(target)]
    far = (block_of(target) + blocks // 2) % blocks
    return jnp.where((block_of(source) == near) | (block_of(source) == far), factor * array, array)


def block_scale(rng, dims, cuts, least, top_value):
    level = 1.0
    for dim, blocks in cuts:
        steps = jax.random.uniform(jax.random.fold_in(jax.random.fold_in(rng, 6), dim), (blocks,), jnp.float32, least / len(cuts), top_value / len(cuts))
        level = level * jnp.repeat(jnp.exp(steps), dims[dim] // blocks).reshape((-1,) + (1,) * (len(dims) - 1 - dim))
    return level


def noise(rng, shape, width, bound, cuts=(), held_as=jnp.bfloat16):
    values = jax.random.normal(rng, shape, jnp.float32) * width
    if len(cuts) > 0:
        values = block_scale(rng, shape, cuts, -0.22, 0.18) * values
    return jnp.clip(values, min=-bound, max=bound).astype(held_as)


def heavy_noise(own_key, dims, deviation, bound, split, heavy, kind=jnp.bfloat16):
    result = deviation * jax.random.normal(own_key, dims, jnp.float32)
    if split:
        result = result * block_scale(own_key, dims, split, -0.22, 0.18)
    return jnp.clip(spiked(result, jax.random.fold_in(own_key, 3), *heavy), -bound, bound).astype(kind)


def setup_inputs(seed: int = 0) -> dict:
    arg_keys = jax.random.split(jax.random.key(seed), 8)
    return {
        "view_left": noise(arg_keys[0], (N, N), N ** -0.5, 0.046875, ((0, 8), (1, 4))),
        "view_right": noise(arg_keys[1], (N, N), 1.0, 6.0, ((0, 8), (1, 4))),
        "view_product": noise(arg_keys[2], (N, N), 1.0, 6.0, ((0, 8), (1, 4))),
        "delta_a_left": noise(arg_keys[3], (N, R), R ** -0.5, 0.25, ((0, 8), (1, 4))),
        "delta_a_right": heavy_noise(arg_keys[4], (N, R), N ** -0.5, 0.0625, ((0, 8), (1, 4)), (0, 1, 8, 2.0)),
        "delta_b_left": noise(arg_keys[5], (N, R), 1.0, 6.0, ((0, 4), (1, 8))),
        "delta_b_right": noise(arg_keys[6], (N, R), R ** -0.5, 0.25, ((0, 4), (1, 8))),
    }


def reference(view_left, view_right, view_product, delta_a_left, delta_a_right, delta_b_left, delta_b_right):
    cross = jnp.dot(delta_a_right.T, delta_b_left, preferred_element_type=jnp.float32).astype(jnp.bfloat16)
    column_sum = jnp.dot(delta_a_right.T, view_right, preferred_element_type=jnp.float32)
    weights_w = (column_sum + jnp.dot(cross, delta_b_right.T, preferred_element_type=jnp.float32)).astype(jnp.bfloat16)
    projected = jnp.dot(view_left, delta_b_left, preferred_element_type=jnp.float32).astype(jnp.bfloat16)
    updated = view_product.astype(jnp.float32) + jnp.dot(delta_a_left, weights_w, preferred_element_type=jnp.float32)
    updated = updated + jnp.dot(projected, delta_b_right.T, preferred_element_type=jnp.float32)
    return updated.astype(jnp.bfloat16)
```

```python
import functools

import jax
import jax.numpy as jnp
from jax import lax
from jax.experimental import pallas as pl
from jax.experimental.pallas import tpu as pltpu
from jax.sharding import PartitionSpec as P

F32 = jnp.float32
BF16 = jnp.bfloat16


def dot(first, second, dims):
    return lax.dot_general(first, second, ((dims[:1], dims[1:]), ((), ())), preferred_element_type=F32)


def final_body(tile, pieces, where_ref, u_ref, near_ref, far_ref, q_near, q_far, *rest):
    y_refs, (c_ref, *_), (o_ref, w_ref) = rest[:pieces], rest[pieces:-2], rest[-2:]
    half = near_ref.shape[0]
    rank = 2 * half
    w_ref[pl.ds(pl.multiple_of(where_ref[0] * half, half), half), :] = near_ref[...]
    w_ref[pl.ds(pl.multiple_of((1 - where_ref[0]) * half, half), half), :] = far_ref[...]
    w_ref[rank : rank + half, :] = q_near[...]
    w_ref[rank + half :, :] = q_far[...]
    for j, y_ref in enumerate(y_refs):
        size = y_ref.shape[0]
        rows = pl.ds(pl.multiple_of((where_ref[1] ^ j) * size, size), size)
        total = jnp.dot(u_ref[rows, :], w_ref[:rank, :], preferred_element_type=F32)
        total = total + jnp.dot(y_ref[...], w_ref[rank:, :], preferred_element_type=F32)
        o_ref[rows, :] = (total + c_ref[rows, :].astype(F32)).astype(BF16)


def final_chunk(where, u, near, far, q_near, q_far, ys, c, out, start, tile):
    rows, rank = u.shape
    half, width = near.shape
    first = start // tile
    here = lambda i, s: (0, i)
    there = lambda i, s: (0, first + i)
    whole = lambda i, s: (0, 0)
    in_specs = [
        pl.BlockSpec((rows, rank), whole),
        pl.BlockSpec((half, tile), here),
        pl.BlockSpec((half, tile), here),
        pl.BlockSpec((half, tile), there),
        pl.BlockSpec((half, tile), there),
        *[pl.BlockSpec(y.shape, whole) for y in ys],
        pl.BlockSpec((rows, tile), there),
    ]
    operands = [where, u, near, far, q_near, q_far, *ys, c]
    aliases = {}
    if out is not None:
        in_specs.append(pl.BlockSpec(memory_space=pl.ANY))
        aliases = {len(operands): 0}
        operands.append(out)
    return pl.pallas_call(
        functools.partial(final_body, tile, len(ys)),
        out_shape=jax.ShapeDtypeStruct(c.shape, BF16),
        grid_spec=pltpu.PrefetchScalarGridSpec(
            num_scalar_prefetch=1,
            grid=(width // tile,),
            in_specs=in_specs,
            out_specs=pl.BlockSpec((rows, tile), there),
            scratch_shapes=[pltpu.VMEM((2 * rank, tile), BF16)],
        ),
        input_output_aliases=aliases,
        compiler_params=pltpu.CompilerParams(vmem_limit_bytes=40 << 20),
        cost_estimate=pl.CostEstimate(
            flops=4 * rows * rank * width, bytes_accessed=4 * rows * width + 4 * rows * rank, transcendentals=0
        ),
        name="final",
    )(*operands)


def per_device(a, b, c_in, u, v, p, q):
    n_row, n_col = lax.axis_size("row"), lax.axis_size("col")
    n_z = n_row // 2
    row, col = lax.axis_index("row"), lax.axis_index("col")
    z, core = row // 2, row % 2
    rows, cols = a.shape
    share, mid = rows // n_col, n_z // 2

    over_col = lambda x, j: lax.ppermute(x, "col", [(i, i ^ j) for i in range(n_col)])
    over_z = lambda x, j: lax.ppermute(x, "row", [(i, i ^ (2 * j)) for i in range(n_row)])
    other = lambda x: lax.ppermute(x, "row", [(i, i ^ 1) for i in range(n_row)])

    def hops(x, moves):
        both = [(s, d) for s, d in moves] + [(n_z - 1 - s, n_z - 1 - d) for s, d in moves]
        return lax.ppermute(x, "row", [(2 * s + k, 2 * d + k) for s, d in both for k in range(2)])

    p_t, q_t = p.T, q.T
    p_near = jnp.concatenate([p_t] + [over_z(p_t, j) for j in range(1, n_z)], 0)
    v_all = jnp.concatenate([v] + [over_col(v, j) for j in range(1, n_col)], 1)
    half = p_near.shape[0]
    rank = 2 * half
    p_far = other(p_near)
    p_all = jnp.concatenate([p_near, p_far], 0)

    v_keep = lax.dynamic_slice_in_dim(v_all, core * half, half, 1)
    v_send = lax.dynamic_slice_in_dim(v_all, (1 - core) * half, half, 1)
    x_send = dot(v_send, b, (0, 0)).astype(BF16)
    x_keep = (dot(v_keep, b, (0, 0)) + other(x_send).astype(F32)).astype(BF16)

    q_one = over_z(q_t, 1)
    if n_z == 4:
        is_mid = (z == 1) | (z == 2)
        inner = hops(jnp.concatenate([q_one, q_t], 0), [(1, 2)])
        outer = hops(inner, [(1, 0)])
        size = q_t.shape[0]
        q_near = jnp.concatenate(
            [q_t, q_one, jnp.where(is_mid, inner[:size], outer[size:]), jnp.where(is_mid, inner[size:], outer[:size])], 0
        )
    else:
        q_near = jnp.concatenate([q_t, q_one] + [over_z(q_t, j) for j in range(2, n_z)], 0)
    q_far = other(q_near)

    size = p_t.shape[0]
    p_here = lax.dynamic_slice_in_dim(p_all, core * rows, rows, 1)
    m_t = dot(p_here, v_all, (1, 0))
    m_near = (m_t[:half] + other(m_t[half:].astype(BF16)).astype(F32)).astype(BF16)
    moved = jnp.zeros_like(m_near)
    for j in range(1, n_z):
        pairs = [((2 * k + e) * n_col + k, (2 * (k ^ j) + e) * n_col + k) for k in range(n_col) for e in range(2)]
        got = lax.ppermute(m_near, ("row", "col"), pairs)
        moved = moved + jnp.concatenate([got[(i ^ j) * size : ((i ^ j) + 1) * size] for i in range(n_z)], 0)
    m_near = jnp.where(z == col, m_near, moved)
    m_all = jnp.concatenate([m_near, other(m_near)], 0)

    u_all = jnp.concatenate([u] + [over_col(u, j) for j in range(1, n_col)], 1)
    y_raw = dot(a, p_all, (1, 1))
    y_part = (y_raw + dot(u_all, m_all, (1, 1))).astype(BF16)
    take = lambda j: lax.dynamic_slice_in_dim(y_part, (col ^ j) * share, share, 0)
    y_sum = take(0).astype(F32)
    for j in range(1, n_col):
        y_sum = y_sum + over_col(take(j), j).astype(F32)
    y_sum = y_sum.astype(BF16)
    ys = [y_sum] + [over_col(y_sum, j) for j in range(1, n_col)]

    where = jnp.stack([core, col]).astype(jnp.int32)
    out, start, tile = None, 0, cols // 8
    for width in (4 * tile, 3 * tile, tile):
        x = x_keep[:, start : start + width]
        for h in range(mid - 1):
            x = x + hops(x, [(h, h + 1)])
        x = x + hops(x, [(mid - 1, mid)])
        for h in reversed(range(mid - 1)):
            got = hops(x, [(h + 1, h)])
            x = jnp.where((z == h) | (z == n_z - 1 - h), got, x)
        out = final_chunk(where, u_all, x, other(x), q_near, q_far, ys, c_in, out, start, tile)
        start += width
    return out


def solution(mesh):
    by_row, by_col = P("row", "col"), P("col", "row")
    return jax.shard_map(
        per_device,
        mesh=mesh,
        in_specs=(by_row, by_row, by_row, by_row, by_row, by_col, by_col),
        out_specs=by_row,
        check_vma=False,
    )
```

```python
import functools

import jax
import jax.numpy as jnp
from jax import lax
from jax.experimental import pallas as pl
from jax.experimental.pallas import tpu as pltpu
from jax.sharding import PartitionSpec as P


F32 = jnp.float32
BF16 = jnp.bfloat16


def whole(shape):
    return pl.BlockSpec(shape, lambda *_: (0,) * len(shape))


def call(body, grid, in_specs, out_specs, out_shape, scratch, flops, moved, operands, aliases={}):
    return pl.pallas_call(
        body,
        out_shape=out_shape,
        grid_spec=pltpu.PrefetchScalarGridSpec(
            num_scalar_prefetch=1, grid=grid, in_specs=in_specs, out_specs=out_specs, scratch_shapes=scratch
        ),
        input_output_aliases=aliases,
        compiler_params=pltpu.CompilerParams(vmem_limit_bytes=48 << 20),
        cost_estimate=pl.CostEstimate(flops=flops, bytes_accessed=moved, transcendentals=0),
    )(*operands)


def join_body(axis, where_ref, *refs):
    *pieces, out = refs
    size = pieces[0].shape[axis]
    for j, piece in enumerate(pieces):
        at = pl.ds(j * size, size)
        out[(at, slice(None)) if axis == 0 else (slice(None), at)] = piece[...]


def join(where, pieces, axis):
    shape = list(pieces[0].shape)
    shape[axis] *= len(pieces)
    shape = tuple(shape)
    steps = 4
    cut = lambda full: (full[0], full[1] // steps) if axis == 0 else (full[0] // steps, full[1])
    at = (lambda i, s: (0, i)) if axis == 0 else (lambda i, s: (i, 0))
    return call(
        functools.partial(join_body, axis), (steps,), [pl.BlockSpec(cut(x.shape), at) for x in pieces],
        pl.BlockSpec(cut(shape), at), jax.ShapeDtypeStruct(shape, BF16), [], 0, 4 * shape[0] * shape[1], [where, *pieces],
    )


def x_body(pieces, widths, where_ref, *refs):
    v_refs, (b_ref, *o_refs, vt_ref) = refs[:pieces], refs[pieces:]
    keeps, sends = o_refs[: len(widths)], o_refs[len(widths) :]
    _, size = v_refs[0].shape
    half, tile = size * pieces // 2, b_ref.shape[1]

    @pl.when(pl.program_id(0) == 0)
    def _():
        for j, v_ref in enumerate(v_refs):
            first = (j // (pieces // 2)) ^ where_ref[0]
            at = pl.multiple_of(first * half + (j % (pieces // 2)) * size, size)
            vt_ref[pl.ds(at, size), :] = v_ref[...].T

    product = jnp.dot(vt_ref[...], b_ref[...], preferred_element_type=F32)
    keep, send = product[:half], product[half:].astype(BF16)
    step = 0
    for keep_ref, send_ref, width in zip(keeps, sends, widths):
        for j in range(width):

            @pl.when(pl.program_id(0) == step)
            def _(keep_ref=keep_ref, send_ref=send_ref, j=j):
                keep_ref[:, j * tile : (j + 1) * tile] = keep
                send_ref[:, j * tile : (j + 1) * tile] = send

            step += 1


def x_part(where, vs, b, first, widths, tile):
    depth, size = vs[0].shape
    half, total = size * len(vs) // 2, sum(widths) * tile
    shapes = [(half, width * tile) for width in widths]
    outs = call(
        functools.partial(x_body, len(vs), widths), (sum(widths),),
        [*[whole(v.shape) for v in vs], pl.BlockSpec((depth, tile), lambda i, s: (0, first + i))],
        [whole(shape) for shape in shapes] * 2,
        [jax.ShapeDtypeStruct(shape, kind) for kind in (F32, BF16) for shape in shapes],
        [pltpu.VMEM((2 * half, depth), BF16)],
        4 * half * depth * total, 2 * depth * total + 6 * half * total, [where, *vs, b],
    )
    return list(zip(outs[: len(widths)], outs[len(widths) :]))


def y_body(pieces, where_ref, *refs):
    p_refs, (a_ref, *o_refs, p_ref) = refs[:pieces], refs[pieces:]
    size = p_refs[0].shape[0]

    @pl.when(pl.program_id(0) == 0)
    def _():
        for j, piece in enumerate(p_refs):
            p_ref[j * size : (j + 1) * size, :] = piece[...]

    product = lax.dot_general(a_ref[...], p_ref[...], (((1,), (1,)), ((), ())), preferred_element_type=F32).astype(BF16)
    for j, o_ref in enumerate(o_refs):

        @pl.when(pl.program_id(0) == j)
        def _(o_ref=o_ref):
            o_ref[...] = product


def y_part(where, ps, a, chunks, last, count):
    size, depth = ps[0].shape
    rank, share = size * len(ps), a.shape[0] // chunks
    return call(
        functools.partial(y_body, len(ps)), (count,),
        [*[whole(p.shape) for p in ps], pl.BlockSpec((share, depth), lambda i, s: (s[1] ^ (last - i), 0))],
        [whole((share, rank))] * count,
        [jax.ShapeDtypeStruct((share, rank), BF16)] * count,
        [pltpu.VMEM((rank, depth), BF16)],
        2 * rank * depth * share * count, 2 * share * count * depth + 2 * rank * depth, [where, *ps, a],
    )


def m_body(pieces, v_pieces, where_ref, *refs):
    p_refs, v_refs, (keep_ref, send_ref, p_ref, v_ref) = refs[:pieces], refs[pieces : pieces + v_pieces], refs[pieces + v_pieces :]
    size, half = p_refs[0].shape[0], keep_ref.shape[0]
    for j, piece in enumerate(p_refs):
        p_ref[j * size : (j + 1) * size, :] = piece[...]
    size = v_refs[0].shape[1]
    for j, piece in enumerate(v_refs):
        v_ref[:, j * size : (j + 1) * size] = piece[...]
    product = jnp.dot(p_ref[...], v_ref[...], preferred_element_type=F32)
    keep_ref[...] = product[:half]
    send_ref[...] = product[half:].astype(BF16)


def m_part(where, ps, vs):
    rows = vs[0].shape[0]
    size = ps[0].shape[0]
    rank = size * len(ps)
    return call(
        functools.partial(m_body, len(ps), len(vs)), (1,),
        [*[pl.BlockSpec((size, rows), lambda i, s: (0, s[0])) for _ in ps], *[whole(v.shape) for v in vs]],
        [whole((rank // 2, rank))] * 2,
        [jax.ShapeDtypeStruct((rank // 2, rank), F32), jax.ShapeDtypeStruct((rank // 2, rank), BF16)],
        [pltpu.VMEM((rank, rows), BF16), pltpu.VMEM((rows, rank), BF16)],
        2 * rank * rank * rows, 4 * rank * rows, [where, *ps, *vs],
    )


def spread_body(count, where_ref, own_ref, *refs):
    *got_refs, o_ref = refs
    size = own_ref.shape[0] // count

    @pl.when(where_ref[1] == where_ref[2])
    def _():
        o_ref[...] = own_ref[...]

    for j, got_ref in enumerate(got_refs, 1):

        @pl.when((where_ref[1] ^ where_ref[2]) == j)
        def _(j=j, got_ref=got_ref):
            for i in range(count):
                o_ref[i * size : (i + 1) * size, :] = got_ref[(i ^ j) * size : ((i ^ j) + 1) * size, :]


def spread(where, own, got):
    return call(
        functools.partial(spread_body, len(got) + 1), (1,), [whole(own.shape)] * (len(got) + 1), whole(own.shape),
        jax.ShapeDtypeStruct(own.shape, BF16), [], 0, 4 * own.shape[0] * own.shape[1], [where, own, *got],
    )


def fix_body(pieces, where_ref, u_ref, m_near, m_far, *refs):
    z_refs, o_ref = refs[:pieces], refs[pieces]
    half, share = m_near.shape[0], z_refs[0].shape[0]
    for j, z_ref in enumerate(z_refs):
        rows = pl.ds(pl.multiple_of((where_ref[1] ^ j) * share, share), share)
        for at, m_ref in ((0, m_near), (half, m_far)):
            cross = lax.dot_general(u_ref[rows, :], m_ref[...], (((1,), (1,)), ((), ())), preferred_element_type=F32)
            o_ref[rows, at : at + half] = (cross + z_ref[:, at : at + half].astype(F32)).astype(BF16)


def fix_part(where, u, m_near, m_far, zs):
    rows, rank = u.shape
    return call(
        functools.partial(fix_body, len(zs)), (1,),
        [whole(x.shape) for x in (u, m_near, m_far, *zs)], whole(u.shape), jax.ShapeDtypeStruct(u.shape, BF16), [],
        2 * rows * rank * rank, 6 * rows * rank, [where, u, m_near, m_far, *zs],
    )


def final_body(pieces, widths, where_ref, u_ref, y_ref, *rest):
    x_refs, rest = rest[: 2 * len(widths)], rest[2 * len(widths) :]
    q_refs, (c_ref, *_), (o_ref, w_ref) = rest[:pieces], rest[pieces:-2], rest[-2:]
    half = x_refs[0].shape[0]
    rank = 2 * half
    first = 0
    for near_ref, far_ref, width in zip(x_refs[::2], x_refs[1::2], widths):

        @pl.when((pl.program_id(0) >= first) & (pl.program_id(0) < first + width))
        def _(near_ref=near_ref, far_ref=far_ref):
            w_ref[pl.ds(pl.multiple_of(where_ref[0] * half, half), half), :] = near_ref[...]
            w_ref[pl.ds(pl.multiple_of((1 - where_ref[0]) * half, half), half), :] = far_ref[...]

        first += width
    size = q_refs[0].shape[0]
    for j, q_ref in enumerate(q_refs):
        w_ref[rank + j * size : rank + (j + 1) * size, :] = q_ref[...]
    total = jnp.dot(u_ref[...], w_ref[:rank, :], preferred_element_type=F32)
    total = total + jnp.dot(y_ref[...], w_ref[rank:, :], preferred_element_type=F32)
    o_ref[...] = (total + c_ref[...].astype(F32)).astype(BF16)


def final_part(where, u, y, xs, qs, c, out, first, tile):
    rows, rank = u.shape
    half = rank // 2
    widths = [near.shape[1] // tile for near, _ in xs]
    there = lambda i, s: (0, first + i)
    in_specs, operands, start = [whole(u.shape), whole(y.shape)], [where, u, y], 0
    for (near, far), width in zip(xs, widths):
        here = lambda i, s, start=start, width=width: (0, jnp.clip(i - start, 0, width - 1))
        in_specs += [pl.BlockSpec((half, tile), here)] * 2
        operands += [near, far]
        start += width
    in_specs += [*[pl.BlockSpec((q.shape[0], tile), there) for q in qs], pl.BlockSpec((rows, tile), there)]
    operands += [*qs, c]
    aliases = {}
    if out is not None:
        in_specs.append(pl.BlockSpec(memory_space=pl.ANY))
        aliases = {len(operands): 0}
        operands.append(out)
    width = start * tile
    return call(
        functools.partial(final_body, len(qs), widths), (start,), in_specs, pl.BlockSpec((rows, tile), there),
        jax.ShapeDtypeStruct(c.shape, BF16), [pltpu.VMEM((2 * rank, tile), BF16)],
        4 * rows * rank * width, 4 * rows * width + 4 * rows * rank, operands, aliases,
    )


FIRST, SECOND, FINAL = (3, 3), (2,), (1, 2)


def per_device(a, b, c_in, u, v, p, q):
    n_row, n_col = lax.axis_size("row"), lax.axis_size("col")
    n_z = n_row // 2
    row, col = lax.axis_index("row"), lax.axis_index("col")
    z, core = row // 2, row % 2
    tile = a.shape[1] // 8
    mid = n_z // 2
    where = jnp.stack([core, col, z]).astype(jnp.int32)

    over_col = lambda x, j: lax.ppermute(x, "col", [(i, i ^ j) for i in range(n_col)])
    over_z = lambda x, j: lax.ppermute(x, "row", [(i, i ^ (2 * j)) for i in range(n_row)])
    other = lambda x: lax.ppermute(x, "row", [(i, i ^ 1) for i in range(n_row)])

    def hops(x, moves):
        both = [(s, d) for s, d in moves] + [(n_z - 1 - s, n_z - 1 - d) for s, d in moves]
        return lax.ppermute(x, "row", [(2 * s + k, 2 * d + k) for s, d in both for k in range(2)])

    def regroup(x, j, count, axis):
        size = x.shape[axis] // count
        return jnp.concatenate([lax.slice_in_dim(x, (i ^ j) * size, ((i ^ j) + 1) * size, axis=axis) for i in range(count)], axis)

    def gather_z(x, direct):
        if direct or n_z != 4:
            return [x] + [over_z(x, j) for j in range(1, n_z)]
        is_mid = (z == 1) | (z == 2)
        x_a, x_b = hops(x, [(0, 1), (1, 0)]), hops(x, [(1, 2)])
        x_c, x_d = hops(x_a, [(1, 2)]), hops(x_b, [(1, 0)])
        x_e = hops(x_c, [(1, 0)])
        return [x, x_a, jnp.where(is_mid, x_c, x_d), jnp.where(is_mid, x_b, x_e)]

    p_near, q_near = gather_z(p.T, True), gather_z(q.T, False)
    vs = [v] + [over_col(v, j) for j in range(1, n_col)]
    us = [u] + [over_col(u, j) for j in range(1, n_col)]
    p_far = [other(x) for x in p_near]
    qs = q_near + [other(x) for x in q_near]
    u_all = join(where, us, 1)

    parts = x_part(where, vs, b, 0, FIRST, tile)
    parts += x_part(where, vs, b, sum(FIRST), SECOND, tile)
    xs = []
    for keep, away in parts:
        got = other(away)
        xs.append((keep + got.astype(F32)).astype(BF16))

    some = n_col // 2
    y_out = list(y_part(where, p_near + p_far, a, n_col, n_col - 1, some))
    y_out += y_part(where, p_near + p_far, a, n_col, some - 1, some)
    y_out = y_out[::-1]
    y_got = [over_col(x, j) for j, x in enumerate(y_out) if j]
    z_sum = y_out[0].astype(F32)
    for x in y_got:
        z_sum = z_sum + x.astype(F32)
    z_sum = z_sum.astype(BF16)
    zs = [z_sum] + [over_col(z_sum, j) for j in range(1, n_col)]

    m_keep, m_send = m_part(where, p_near + p_far, vs)
    m_got = other(m_send)
    m = (m_keep + m_got.astype(F32)).astype(BF16)
    moved = []
    for j in range(1, n_z):
        pairs = [((2 * k + e) * n_col + k, (2 * (k ^ j) + e) * n_col + k) for k in range(n_col) for e in range(2)]
        moved.append(lax.ppermute(m, ("row", "col"), pairs))
    m = spread(where, m, moved)
    step = 1
    while step < n_col:
        got = over_col(m, step)
        m = m + regroup(got, step, n_col, 1)
        step *= 2
    m_far = other(m)
    y_all = fix_part(where, u_all, m, m_far, zs)

    ready = []
    for x in xs:
        for h in range(mid - 1):
            got = hops(x, [(h, h + 1)])
            x = x + got
        got = hops(x, [(mid - 1, mid)])
        x = x + got
        for h in reversed(range(mid - 1)):
            got = hops(x, [(h + 1, h)])
            x = jnp.where((z == h) | (z == n_z - 1 - h), got, x)
        ready.append((x, other(x)))
    out, first = None, 0
    for count in FINAL:
        now, ready = ready[:count], ready[count:]
        out = final_part(where, u_all, y_all, now, qs, c_in, out, first, tile)
        first += sum(x.shape[1] for x, _ in now) // tile
    return out


def solution(mesh):
    by_row, by_col = P("row", "col"), P("col", "row")
    return jax.shard_map(
        per_device,
        mesh=mesh,
        in_specs=(by_row, by_row, by_row, by_row, by_row, by_col, by_col),
        out_specs=by_row,
        check_vma=False,
    )
```
